32 devices in a mesh: parts: 2 (over x), row: 16 (over z, y, core).
Axes of the slice: x: 2, y: 2, z: 4, core: 2. Of those that a mesh axis runs over, the one named last changes fastest.
Arguments:
- latent: bfloat16 [64, 256, 512], P(('parts', 'row')), parts along dimension 0, may hold values from -6 to 6
- conv_first: bfloat16 [3, 3, 512, 512], P(None, None, 'row'), may hold values from -0.09375 to 0.09375
- conv_second: bfloat16 [3, 3, 512, 512], P(None, None, 'row'), may hold values from -0.09375 to 0.09375
- w_query: bfloat16 [512, 512], replicated
- w_key: bfloat16 [512, 512], replicated
- w_value: bfloat16 [512, 512], replicated, may hold values from -0.25 to 0.25
- w_out: bfloat16 [512, 512], replicated, may hold values from -0.25 to 0.25
- w_in: bfloat16 [512, 2048], replicated, may hold values from -0.25 to 0.25
- w_down: bfloat16 [2048, 512], replicated, may hold values from -0.125 to 0.125
- conv_up: bfloat16 [3, 3, 512, 512], P(None, None, 'row'), may hold values from -0.09375 to 0.09375
Outputs:
- latent_out: bfloat16 [64, 256, 512], P(('parts', 'row')), parts along dimension 0
- upsampled: bfloat16 [64, 256, 512], P('parts', 'row'), parts along dimension 0
The draws below stay inside these ranges and needn't reach their ends.
There are 2 independent parts, one for each index of `parts`. The reference program is written for one: setup_inputs(seed, part) draws one part's arguments, and reference() takes and returns one part's arrays. A program takes and returns all parts, laid end to end along the dimension named above; an argument that names none is the same for every part. Nothing has to cross between parts.
All inputs are finite; a program needn't handle non-finite values.
Results may differ from the reference program's by a relative error of at most 0.015.
Values may be sent and summed in bfloat16 or wider, within the bound.
A program may use at most 128 MiB of HBM per device.

```python
import math
import jax
import jax.numpy as jnp
from jax import lax

C = 512
HEADS = 8
HD = 64
FF = 2048
GRID = 16
W = 256
H = 32


def common_matrix(key):
    return jax.random.normal(jax.random.fold_in(key, 7), (C, C), jnp.float32)


def draw_w_query(key, part):
    common = common_matrix(key)
    return (common * (1.0 / math.sqrt(C))).astype(jnp.bfloat16)


def draw_w_key(key, part):
    private = jax.random.normal(jax.random.fold_in(key, 8), (C, C), jnp.float32)
    return (private * (1.0 / math.sqrt(C))).astype(jnp.bfloat16)


def level_of(key, extent, cuts, smallest, high):
    def one(position, parts):
        steps = jax.random.uniform(jax.random.fold_in(jax.random.fold_in(key, 6), position), (parts,), jnp.float32, smallest / len(cuts), high / len(cuts))
        return jnp.repeat(jnp.exp(steps), extent[position] // parts).reshape((-1,) + (1,) * (len(extent) - position - 1))

    factor_of = one(*cuts[0])
    for cut in cuts[1:]:
        factor_of = factor_of * one(*cut)
    return factor_of


def centred(rng, extent, spread, bound, cuts=(), kind=jnp.bfloat16):
    loudness = level_of(rng, extent, cuts, -0.22, 0.18) if cuts else 1.0
    drawn = jax.random.normal(rng, extent, jnp.float32) * spread * loudness
    return jnp.minimum(jnp.maximum(drawn, -bound), bound).astype(kind)


def setup_inputs(seed: int = 0, part: int = 0) -> dict:
    keys = jax.random.split(jax.random.key(seed), 11)
    part_keys = jax.random.split(jax.random.fold_in(keys[10], part), 11)
    return {
        "latent": centred(part_keys[0], (H, W, C), 1.0, 6.0, ((0, 16),)),
        "conv_first": centred(keys[1], (3, 3, C, C), (9 * C) ** -0.5, 0.09375, ((2, 16),)),
        "conv_second": centred(keys[2], (3, 3, C, C), (9 * C) ** -0.5, 0.09375, ((2, 16),)),
        "w_query": draw_w_query(jax.random.fold_in(keys[10], 71), part),
        "w_key": draw_w_key(jax.random.fold_in(keys[10], 71), part),
        "w_value": centred(keys[5], (C, C), C ** -0.5, 0.25),
        "w_out": centred(keys[6], (C, C), C ** -0.5, 0.25),
        "w_in": centred(keys[7], (C, FF), C ** -0.5, 0.25),
        "w_down": centred(keys[8], (FF, C), FF ** -0.5, 0.125),
        "conv_up": centred(keys[9], (3, 3, C, C), (9 * C) ** -0.5, 0.09375, ((2, 16),)),
    }


def rms_round(values):
    meansq = lax.optimization_barrier(jnp.mean(values * values, axis=-1, keepdims=True))
    return (values * lax.rsqrt(meansq + 1e-06)).astype(jnp.bfloat16)

def convolve(field, kernel):
    height, breadth, channels = field.shape
    padded = jnp.pad(field, ((1, 1), (1, 1), (0, 0)))
    running = jnp.zeros((height * breadth, kernel.shape[3]), jnp.float32)
    for shift_row in range(3):
        for shift_col in range(3):
            window = padded[shift_row:shift_row + height, shift_col:shift_col + breadth].reshape(-1, channels)
            running = running + jnp.dot(window, kernel[shift_row, shift_col], preferred_element_type=jnp.float32)
    return running.reshape(height, breadth, kernel.shape[3])

def softmax_round(scores):
    highest = lax.optimization_barrier(jnp.max(scores, axis=-1, keepdims=True))
    lifted = jnp.exp(scores - highest)
    return (lifted / lax.optimization_barrier(jnp.sum(lifted, axis=-1, keepdims=True))).astype(jnp.bfloat16)

def reference(latent, conv_first, conv_second, w_query, w_key, w_value, w_out, w_in, w_down, conv_up):
    current = latent
    for kernel in (conv_first, conv_second):
        active = jax.nn.gelu(current.astype(jnp.float32)).astype(jnp.bfloat16)
        current = (current.astype(jnp.float32) + convolve(active, kernel)).astype(jnp.bfloat16)
    height, breadth, channels = current.shape
    normed = rms_round(current.astype(jnp.float32)).reshape(-1, channels)
    queries = jnp.dot(normed, w_query, preferred_element_type=jnp.float32).astype(jnp.bfloat16)
    keys_all = jnp.dot(normed, w_key, preferred_element_type=jnp.float32).astype(jnp.bfloat16)
    values_all = jnp.dot(normed, w_value, preferred_element_type=jnp.float32).astype(jnp.bfloat16)
    band_rows = height // GRID
    band_cols = breadth // GRID
    scale = HD ** (-0.5)

    def windows(tensor):
        return tensor.reshape(GRID, band_rows, GRID, band_cols, HEADS, HD).transpose(1, 0, 2, 3, 4, 5)

    def attend(blocks):
        query_block, key_block, value_block = blocks
        scores = jnp.einsum('abchd,efchd->chabef', query_block.astype(jnp.float32), key_block.astype(jnp.float32)) * scale
        scores = scores.reshape(band_cols, HEADS, GRID * GRID, GRID * GRID)
        probs = softmax_round(scores).reshape(band_cols, HEADS, GRID, GRID, GRID, GRID)
        output = jnp.einsum('chabef,efchd->abchd', probs.astype(jnp.float32), value_block.astype(jnp.float32))
        return output.astype(jnp.bfloat16)
    attended = lax.map(attend, (windows(queries), windows(keys_all), windows(values_all)))
    attended = attended.transpose(1, 0, 2, 3, 4, 5).reshape(-1, channels)
    projected = jnp.dot(attended, w_out, preferred_element_type=jnp.float32).reshape(height, breadth, channels)
    current = (current.astype(jnp.float32) + projected).astype(jnp.bfloat16)
    normed_two = rms_round(current.astype(jnp.float32)).reshape(-1, channels)
    hidden = jax.nn.gelu(jnp.dot(normed_two, w_in, preferred_element_type=jnp.float32)).astype(jnp.bfloat16)
    lowered = jnp.dot(hidden, w_down, preferred_element_type=jnp.float32).reshape(height, breadth, channels)
    latent_out = (current.astype(jnp.float32) + lowered).astype(jnp.bfloat16)
    central = latent_out[height // 4:3 * height // 4, breadth // 4:3 * breadth // 4]
    doubled = jnp.repeat(jnp.repeat(central, 2, axis=0), 2, axis=1)
    upsampled = convolve(doubled, conv_up).astype(jnp.bfloat16)
    return (latent_out, upsampled)
```

```python
import functools

import jax
import jax.numpy as jnp
from jax import lax
from jax.experimental import pallas as pl
from jax.experimental.pallas import tpu as pltpu
from jax.sharding import PartitionSpec as P

HD = 64
GRID = 16
F32 = jnp.float32
BF16 = jnp.bfloat16


def gelu(values):
    return jax.nn.gelu(values.astype(F32)).astype(BF16)


def rms_round(values):
    meansq = jnp.mean(values * values, axis=-1, keepdims=True)
    return (values * lax.rsqrt(meansq + 1e-06)).astype(BF16)


def dot(a, b):
    return jnp.dot(a, b, preferred_element_type=F32)


def conv_body(rows, top_ref, mid_ref, bot_ref, k_ref, res_ref, o_ref, act_ref):
    @pl.when(pl.program_id(0) == 0)
    def _():
        act_ref[0] = gelu(top_ref[0])
        for i in range(rows):
            act_ref[i + 1] = gelu(mid_ref[i])
        act_ref[rows + 1] = gelu(bot_ref[0])

    cols = act_ref.shape[1]
    width = k_ref.shape[3]
    col = lax.broadcasted_iota(jnp.int32, (cols, width), 0)
    for i in range(rows):
        sums = []
        for v in range(3):
            s = dot(act_ref[i], k_ref[0, v])
            s = s + dot(act_ref[i + 1], k_ref[1, v])
            s = s + dot(act_ref[i + 2], k_ref[2, v])
            sums.append(s)
        left = jnp.where(col == 0, 0.0, pltpu.roll(sums[0], 1, 0))
        right = jnp.where(col == cols - 1, 0.0, pltpu.roll(sums[2], cols - 1, 0))
        total = sums[1] + left + right
        o_ref[i] = (res_ref[i].astype(F32) + total).astype(BF16)


def conv_block(top, mid, bot, kernel, residual):
    rows, cols, channels = mid.shape
    out_channels = kernel.shape[3]
    width = min(256, out_channels)
    whole = lambda n: pl.BlockSpec((n, cols, channels), lambda b: (0, 0, 0))
    part = pl.BlockSpec((rows, cols, width), lambda b: (0, 0, b))
    return pl.pallas_call(
        functools.partial(conv_body, rows),
        grid=(out_channels // width,),
        in_specs=[
            whole(1),
            whole(rows),
            whole(1),
            pl.BlockSpec((3, 3, channels, width), lambda b: (0, 0, 0, b)),
            part,
        ],
        out_specs=part,
        out_shape=jax.ShapeDtypeStruct((rows, cols, out_channels), BF16),
        scratch_shapes=[pltpu.VMEM((rows + 2, cols, channels), BF16)],
        compiler_params=pltpu.CompilerParams(vmem_limit_bytes=48 << 20),
        name="conv_block",
        cost_estimate=pl.CostEstimate(
            flops=18 * rows * cols * channels * out_channels,
            bytes_accessed=18 * channels * out_channels,
            transcendentals=0,
        ),
    )(top, mid, bot, kernel, residual)


def window_body(x_ref, wq_ref, wk_ref, wv_ref, wo_ref, wi_ref, wd_ref, o_ref, att_ref):
    shape = x_ref.shape
    channels = shape[-1]
    cells = shape[0] * shape[2]
    x = x_ref[:, 0].reshape(cells, channels).astype(F32)
    normed = rms_round(x)
    queries = dot(normed, wq_ref[...]).astype(BF16)
    keys = dot(normed, wk_ref[...]).astype(BF16)
    values = dot(normed, wv_ref[...]).astype(BF16)
    pair = 2 * HD
    lane = lax.broadcasted_iota(jnp.int32, (cells, pair), 1)
    zero = jnp.zeros((cells, pair), BF16)
    for p in range(channels // pair):
        q = queries[:, p * pair : (p + 1) * pair]
        k = keys[:, p * pair : (p + 1) * pair]
        v = values[:, p * pair : (p + 1) * pair]
        out = None
        for half in range(2):
            own = (lane < HD) if half == 0 else (lane >= HD)
            scores = lax.dot_general(
                jnp.where(own, q, zero), k, (((1,), (1,)), ((), ())), preferred_element_type=F32
            ) * HD ** (-0.5)
            lifted = jnp.exp(scores - jnp.max(scores, axis=-1, keepdims=True))
            probs = (lifted * (1.0 / jnp.sum(lifted, axis=-1, keepdims=True))).astype(BF16)
            term = dot(probs, jnp.where(own, v, zero))
            out = term if out is None else out + term
        att_ref[:, p * pair : (p + 1) * pair] = out.astype(BF16)
    y3 = (x + dot(att_ref[...], wo_ref[...])).astype(BF16).astype(F32)
    hidden = gelu(dot(rms_round(y3), wi_ref[...]))
    result = (y3 + dot(hidden, wd_ref[...])).astype(BF16)
    o_ref[:, 0] = result.reshape(shape[0], shape[2], channels)


def window_block(x, *weights):
    grid_cells, bands, others, channels = x.shape
    part = pl.BlockSpec((grid_cells, 1, others, channels), lambda b: (0, b, 0, 0))
    whole = [pl.BlockSpec(w.shape, lambda b: (0, 0), pipeline_mode=pl.Buffered(1)) for w in weights]
    cells = grid_cells * others
    work = sum(w.size for w in weights)
    return pl.pallas_call(
        window_body,
        grid=(bands,),
        in_specs=[part] + whole,
        out_specs=part,
        out_shape=jax.ShapeDtypeStruct(x.shape, BF16),
        scratch_shapes=[pltpu.VMEM((cells, channels), BF16)],
        compiler_params=pltpu.CompilerParams(vmem_limit_bytes=48 << 20),
        name="window_block",
        cost_estimate=pl.CostEstimate(
            flops=2 * bands * cells * (work + 2 * cells * channels),
            bytes_accessed=2 * work,
            transcendentals=bands * cells * (cells * channels // HD),
        ),
    )(x, *weights)


def up_body(d_ref, k_ref, o_ref):
    _, rows, cols, channels = d_ref.shape
    width = k_ref.shape[3]
    sums = []
    for u in range(3):
        s = None
        for v in range(3):
            term = dot(d_ref[v].reshape(rows * cols, channels), k_ref[u, v])
            s = term if s is None else s + term
        sums.append(s.reshape(rows, cols, width))
    for i in range(rows):
        even = sums[1][i] + sums[2][i]
        if i > 0:
            even = even + sums[0][i - 1]
        odd = sums[0][i] + sums[1][i]
        if i < rows - 1:
            odd = odd + sums[2][i + 1]
        o_ref[2 * i] = even.astype(BF16)
        o_ref[2 * i + 1] = odd.astype(BF16)


def up_block(doubled, kernel):
    _, rows, cols, channels = doubled.shape
    out_channels = kernel.shape[3]
    width = min(256, out_channels)
    return pl.pallas_call(
        up_body,
        grid=(out_channels // width,),
        in_specs=[
            pl.BlockSpec(doubled.shape, lambda b: (0, 0, 0, 0)),
            pl.BlockSpec((3, 3, channels, width), lambda b: (0, 0, 0, b)),
        ],
        out_specs=pl.BlockSpec((2 * rows, cols, width), lambda b: (0, 0, b)),
        out_shape=jax.ShapeDtypeStruct((2 * rows, cols, out_channels), BF16),
        compiler_params=pltpu.CompilerParams(vmem_limit_bytes=48 << 20),
        name="up_block",
        cost_estimate=pl.CostEstimate(
            flops=18 * rows * cols * channels * out_channels,
            bytes_accessed=18 * channels * out_channels,
            transcendentals=0,
        ),
    )(doubled, kernel)


def whole_kernel(kernel_piece):
    return lax.all_gather(kernel_piece, "row", axis=2, tiled=True)


def edge_rows(value):
    size = lax.axis_size("row")
    up = [(i, i + 1) for i in range(size - 1)]
    down = [(j, i) for i, j in up]
    before = lax.ppermute(value[-1:], "row", up)
    after = lax.ppermute(value[:1], "row", down)
    return before, after


def convolve(padded, kernel, out_rows, out_cols):
    total = 0.0
    for u in range(3):
        for v in range(3):
            taps = padded[u : u + out_rows, v : v + out_cols]
            total = total + dot(taps.reshape(-1, taps.shape[2]), kernel[u, v])
    return total


def central_by_rows(latent_out, devices):
    grid_rows, grid_cols, channels = latent_out.shape
    central = latent_out[:, grid_cols // 4 : 3 * grid_cols // 4]
    central_cols = central.shape[1]
    slice_cols = central_cols // devices
    padded = jnp.pad(central, ((0, 0), (1, 1), (0, 0)))
    left = padded[:, :central_cols].reshape(grid_rows, devices, slice_cols, channels)
    first = padded[:, slice_cols::slice_cols]
    second = padded[:, slice_cols + 1 :: slice_cols]
    outgoing = jnp.concatenate([left, first[:, :, None], second[:, :, None]], axis=2)
    arrived = lax.all_to_all(outgoing, "row", split_axis=1, concat_axis=0, tiled=True)
    total_rows = arrived.shape[0]
    return arrived[total_rows // 4 : 3 * total_rows // 4, 0]


def central_by_windows(windows):
    grid_cells, bands, others, channels = windows.shape
    low, high = grid_cells // 4, 3 * grid_cells // 4
    mine = lax.axis_index("row")
    central = windows[low:high, :, others // 4 : 3 * others // 4]
    rows = (high - low) * bands
    central = central.reshape(rows, -1, channels).transpose(1, 0, 2)
    blank = jnp.zeros_like(central[:1])
    even = jnp.where(mine == grid_cells - 1, jnp.concatenate([blank, central[:-1]]), central)
    odd = jnp.where(mine == 0, jnp.concatenate([central[1:], blank]), central)
    outgoing = jnp.stack([even, odd], axis=1).reshape(-1, rows, channels)
    arrived = lax.all_to_all(outgoing, "row", split_axis=0, concat_axis=0, tiled=True)
    half = grid_cells // 2
    if_even = jnp.concatenate([arrived[-1:], arrived[: half + 1]])
    if_odd = jnp.concatenate([arrived[half - 1 :], arrived[:1]])
    return jnp.where(mine % 2 == 0, if_even, if_odd).transpose(1, 0, 2)


def on_device(
    latent, conv_first, conv_second, w_query, w_key, w_value, w_out, w_in, w_down, conv_up
):
    devices = lax.axis_size("row")
    grid_rows, grid_cols, channels = latent.shape
    current = latent
    for piece in (conv_first, conv_second):
        before, after = edge_rows(current)
        current = conv_block(before, current, after, whole_kernel(piece), current)
    up_kernel = whole_kernel(conv_up)

    step = devices // GRID
    groups = None
    if step > 1:
        groups = [[j + step * c for c in range(GRID)] for j in range(step)]
    exchange = functools.partial(
        lax.all_to_all,
        axis_name="row",
        split_axis=0,
        concat_axis=0,
        tiled=True,
        axis_index_groups=groups,
    )
    by_column = current.reshape(grid_rows, -1, GRID, channels).transpose(2, 0, 1, 3)
    windows = window_block(
        exchange(by_column), w_query, w_key, w_value, w_out, w_in, w_down
    )
    fast = step == 1 and grid_cols == GRID * GRID and channels % 128 == 0
    if fast:
        framed = central_by_windows(windows)
    latent_out = exchange(windows).transpose(1, 2, 0, 3).reshape(grid_rows, grid_cols, channels)
    if not fast:
        framed = central_by_rows(latent_out, devices)
    cols = framed.shape[1] - 2
    doubled = jnp.repeat(framed, 2, axis=1)[:, 1:-1]
    if fast:
        taps = jnp.stack([doubled[:, v : v + 2 * cols] for v in range(3)])
        return latent_out, up_block(taps, up_kernel)
    doubled = jnp.pad(jnp.repeat(doubled, 2, axis=0), ((1, 1), (0, 0), (0, 0)))
    total_rows = doubled.shape[0] - 2
    upsampled = convolve(doubled, up_kernel, total_rows, 2 * cols).astype(BF16)
    return latent_out, upsampled.reshape(total_rows, 2 * cols, channels)


def solution(mesh):
    placed = (
        P(("parts", "row"), None, None),
        P(None, None, "row", None),
        P(None, None, "row", None),
        P(),
        P(),
        P(),
        P(),
        P(),
        P(),
        P(None, None, "row", None),
    )
    return jax.shard_map(
        on_device,
        mesh=mesh,
        in_specs=placed,
        out_specs=(P(("parts", "row"), None, None), P("parts", "row", None)),
        check_vma=False,
    )
```

```python
import functools

import jax
import jax.numpy as jnp
from jax import lax
from jax.experimental import pallas as pl
from jax.experimental.pallas import tpu as pltpu
from jax.sharding import PartitionSpec as P

HD = 64
GRID = 16
F32 = jnp.float32
BF16 = jnp.bfloat16


def gelu(values):
    return jax.nn.gelu(values.astype(F32)).astype(BF16)


def rms_round(values):
    meansq = jnp.mean(values * values, axis=-1, keepdims=True)
    return (values * lax.rsqrt(meansq + 1e-06)).astype(BF16)


def dot(a, b):
    return jnp.dot(a, b, preferred_element_type=F32)


def conv_body(rows, top_ref, mid_ref, bot_ref, k_ref, res_ref, o_ref, act_ref):
    @pl.when(pl.program_id(0) == 0)
    def _():
        act_ref[0] = gelu(top_ref[0])
        for i in range(rows):
            act_ref[i + 1] = gelu(mid_ref[i])
        act_ref[rows + 1] = gelu(bot_ref[0])

    cols = act_ref.shape[1]
    width = k_ref.shape[3]
    col = lax.broadcasted_iota(jnp.int32, (cols, width), 0)
    for i in range(rows):
        sums = []
        for v in range(3):
            s = dot(act_ref[i], k_ref[0, v])
            s = s + dot(act_ref[i + 1], k_ref[1, v])
            s = s + dot(act_ref[i + 2], k_ref[2, v])
            sums.append(s)
        left = jnp.where(col == 0, 0.0, pltpu.roll(sums[0], 1, 0))
        right = jnp.where(col == cols - 1, 0.0, pltpu.roll(sums[2], cols - 1, 0))
        total = sums[1] + left + right
        o_ref[i] = (res_ref[i].astype(F32) + total).astype(BF16)


def conv_block(top, mid, bot, kernel, residual):
    rows, cols, channels = mid.shape
    out_channels = kernel.shape[3]
    width = min(256, out_channels)
    whole = lambda n: pl.BlockSpec((n, cols, channels), lambda b: (0, 0, 0))
    part = pl.BlockSpec((rows, cols, width), lambda b: (0, 0, b))
    return pl.pallas_call(
        functools.partial(conv_body, rows),
        grid=(out_channels // width,),
        in_specs=[
            whole(1),
            whole(rows),
            whole(1),
            pl.BlockSpec((3, 3, channels, width), lambda b: (0, 0, 0, b)),
            part,
        ],
        out_specs=part,
        out_shape=jax.ShapeDtypeStruct((rows, cols, out_channels), BF16),
        scratch_shapes=[pltpu.VMEM((rows + 2, cols, channels), BF16)],
        compiler_params=pltpu.CompilerParams(vmem_limit_bytes=48 << 20),
        name="conv_block",
        cost_estimate=pl.CostEstimate(
            flops=18 * rows * cols * channels * out_channels,
            bytes_accessed=18 * channels * out_channels,
            transcendentals=0,
        ),
    )(top, mid, bot, kernel, residual)


def window_body(x_ref, wq_ref, wk_ref, wv_ref, wo_ref, wi_ref, wd_ref, o_ref, att_ref):
    shape = x_ref.shape
    channels = shape[-1]
    cells = shape[0] * shape[2]
    x = x_ref[:, 0].reshape(cells, channels).astype(F32)
    normed = rms_round(x)
    queries = dot(normed, wq_ref[...]).astype(BF16)
    keys = dot(normed, wk_ref[...]).astype(BF16)
    values = dot(normed, wv_ref[...]).astype(BF16)
    pair = 2 * HD
    lane = lax.broadcasted_iota(jnp.int32, (cells, pair), 1)
    zero = jnp.zeros((cells, pair), BF16)
    for p in range(channels // pair):
        q = queries[:, p * pair : (p + 1) * pair]
        k = keys[:, p * pair : (p + 1) * pair]
        v = values[:, p * pair : (p + 1) * pair]
        out = None
        for half in range(2):
            own = (lane < HD) if half == 0 else (lane >= HD)
            scores = lax.dot_general(
                jnp.where(own, q, zero), k, (((1,), (1,)), ((), ())), preferred_element_type=F32
            ) * HD ** (-0.5)
            lifted = jnp.exp(scores - jnp.max(scores, axis=-1, keepdims=True))
            probs = (lifted * (1.0 / jnp.sum(lifted, axis=-1, keepdims=True))).astype(BF16)
            term = dot(probs, jnp.where(own, v, zero))
            out = term if out is None else out + term
        att_ref[:, p * pair : (p + 1) * pair] = out.astype(BF16)
    y3 = (x + dot(att_ref[...], wo_ref[...])).astype(BF16).astype(F32)
    hidden = gelu(dot(rms_round(y3), wi_ref[...]))
    result = (y3 + dot(hidden, wd_ref[...])).astype(BF16)
    o_ref[:, 0] = result.reshape(shape[0], shape[2], channels)


def window_block(x, *weights):
    grid_cells, bands, others, channels = x.shape
    part = pl.BlockSpec((grid_cells, 1, others, channels), lambda b: (0, b, 0, 0))
    whole = [pl.BlockSpec(w.shape, lambda b: (0, 0), pipeline_mode=pl.Buffered(1)) for w in weights]
    cells = grid_cells * others
    work = sum(w.size for w in weights)
    return pl.pallas_call(
        window_body,
        grid=(bands,),
        in_specs=[part] + whole,
        out_specs=part,
        out_shape=jax.ShapeDtypeStruct(x.shape, BF16),
        scratch_shapes=[pltpu.VMEM((cells, channels), BF16)],
        compiler_params=pltpu.CompilerParams(vmem_limit_bytes=48 << 20),
        name="window_block",
        cost_estimate=pl.CostEstimate(
            flops=2 * bands * cells * (work + 2 * cells * channels),
            bytes_accessed=2 * work,
            transcendentals=bands * cells * (cells * channels // HD),
        ),
    )(x, *weights)


def up_body(d_ref, k_ref, o_ref):
    _, rows, cols, channels = d_ref.shape
    width = k_ref.shape[3]
    sums = []
    for u in range(3):
        s = None
        for v in range(3):
            term = dot(d_ref[v].reshape(rows * cols, channels), k_ref[u, v])
            s = term if s is None else s + term
        sums.append(s.reshape(rows, cols, width))
    for i in range(rows):
        even = sums[1][i] + sums[2][i]
        if i > 0:
            even = even + sums[0][i - 1]
        odd = sums[0][i] + sums[1][i]
        if i < rows - 1:
            odd = odd + sums[2][i + 1]
        o_ref[2 * i] = even.astype(BF16)
        o_ref[2 * i + 1] = odd.astype(BF16)


def up_block(doubled, kernel):
    _, rows, cols, channels = doubled.shape
    out_channels = kernel.shape[3]
    width = min(256, out_channels)
    return pl.pallas_call(
        up_body,
        grid=(out_channels // width,),
        in_specs=[
            pl.BlockSpec(doubled.shape, lambda b: (0, 0, 0, 0)),
            pl.BlockSpec((3, 3, channels, width), lambda b: (0, 0, 0, b)),
        ],
        out_specs=pl.BlockSpec((2 * rows, cols, width), lambda b: (0, 0, b)),
        out_shape=jax.ShapeDtypeStruct((2 * rows, cols, out_channels), BF16),
        compiler_params=pltpu.CompilerParams(vmem_limit_bytes=48 << 20),
        name="up_block",
        cost_estimate=pl.CostEstimate(
            flops=18 * rows * cols * channels * out_channels,
            bytes_accessed=18 * channels * out_channels,
            transcendentals=0,
        ),
    )(doubled, kernel)


def whole_kernel(kernel_piece):
    return lax.all_gather(kernel_piece, "row", axis=2, tiled=True)


def gather_body(count, nz, *refs):
    pieces, wholes, owns = refs[:count], refs[count : 2 * count], refs[2 * count : 3 * count]
    load_sem, keep_sem, zs, zr, ys, yr, xs, xr, cs, cr = refs[3 * count :]
    index, part = lax.axis_index("row"), lax.axis_index("parts")
    core, y, z = index % 2, (index // 2) % 2, index // 4
    parity = part % 2
    taps, rows, _ = pieces[0].shape
    half = rows // 2
    zero = nz - 1

    def device(z_, y_, core_, part_):
        return {"parts": part_, "row": (z_ * 2 + y_) * 2 + core_}

    def place(ref, z_, y_, t):
        base = ((z_ * 2 + y_) * 2 + core) * rows
        size = rows
        if t is not None:
            base = base + ((parity + t) % 2) * half
            size = half
        return ref.at[:, pl.ds(pl.multiple_of(base, size), size)]

    def source(m, d, t):
        if d != 0:
            return place(wholes[m], z - d, y, t)
        if t is None:
            return pieces[m]
        return pieces[m].at[:, pl.ds(pl.multiple_of(((parity + t) % 2) * half, half), half)]

    def remote(src, dst, send, recv, to):
        return pltpu.make_async_remote_copy(
            src_ref=src,
            dst_ref=dst,
            send_sem=send,
            recv_sem=recv,
            device_id=to,
            device_id_type=pl.DeviceIdType.MESH,
        )

    def z_copy(m, d, t, way):
        slot = d + way + zero
        return remote(
            source(m, d, t),
            place(wholes[m], z - d, y, t),
            zs.at[m, slot, t],
            zr.at[m, slot, t],
            device(z + way, y, core, part),
        )

    def z_arrival(m, d, t):
        here = place(wholes[m], z - d, y, t)
        way = 1 if d > 0 else -1
        slot = d + zero
        return remote(
            here, here, zs.at[m, slot, t], zr.at[m, slot, t], device(z - way, y, core, part)
        )

    def y_copy(m, d):
        slot = d + zero
        return remote(
            source(m, d, 0),
            place(wholes[m], z - d, y, 0),
            ys.at[m, slot],
            yr.at[m, slot],
            device(z, 1 - y, core, part),
        )

    def y_arrival(m, d):
        here = place(wholes[m], z - d, 1 - y, 0)
        slot = d + zero
        return remote(here, here, ys.at[m, slot], yr.at[m, slot], device(z, 1 - y, core, part))

    def x_copy(m, d):
        here = place(wholes[m], z - d, 1 - y, 0)
        slot = d + zero
        to = device(z, y, core, part + 1 - 2 * parity)
        return remote(here, here, xs.at[m, slot], xr.at[m, slot], to)

    def x_arrival(m, d):
        here = place(wholes[m], z - d, 1 - y, 1)
        slot = d + zero
        to = device(z, y, core, part + 1 - 2 * parity)
        return remote(here, here, xs.at[m, slot], xr.at[m, slot], to)

    def c_copy(m, column, d):
        slot = d + zero
        to = device(z, y, 1 - core, part)
        if column == 0:
            src, dst = source(m, d, None), place(wholes[m], z - d, y, None)
        else:
            src = place(wholes[m], z - d, 1 - y, None)
            dst = src
        return remote(src, dst, cs.at[m, column, slot], cr.at[m, column, slot], to)

    def c_arrival(m, column, d):
        slot = d + zero
        y_ = y if column == 0 else 1 - y
        base = ((z - d) * 2 + y_) * 2 + 1 - core
        here = wholes[m].at[:, pl.ds(pl.multiple_of(base * rows, rows), rows)]
        to = device(z, y, 1 - core, part)
        return remote(here, here, cs.at[m, column, slot], cr.at[m, column, slot], to)

    def when(condition, action):
        if condition is None:
            action()
        else:
            pl.when(condition)(action)

    def valid(d):
        if d == 0:
            return None
        return z >= d if d > 0 else z - d <= nz - 1

    def ahead(way):
        return z < nz - 1 if way > 0 else z > 0

    def both(distance):
        return (0,) if distance == 0 else (distance, -distance)

    barrier = pltpu.get_barrier_semaphore()

    def greet(to):
        pl.semaphore_signal(
            barrier, inc=1, device_id=to, device_id_type=pl.DeviceIdType.MESH
        )

    greet(device(z, 1 - y, core, part))
    greet(device(z, y, 1 - core, part))
    greet(device(z, y, core, part + 1 - 2 * parity))
    for way in (1, -1):
        when(ahead(way), functools.partial(greet, device(z + way, y, core, part)))
    pl.semaphore_wait(barrier, 3 + jnp.minimum(z, 1) + jnp.minimum(nz - 1 - z, 1))

    loads = [
        pltpu.make_async_copy(pieces[m], owns[m], load_sem.at[m]) for m in range(count)
    ]
    keeps = [
        pltpu.make_async_copy(owns[m], place(wholes[m], z, y, None), keep_sem.at[m])
        for m in range(count)
    ]
    for m in range(count):
        for t in range(2):
            for way in (1, -1):
                when(ahead(way), lambda: z_copy(m, 0, t, way).start())
        y_copy(m, 0).start()
        c_copy(m, 0, 0).start()
        loads[m].start()
    for m in range(count):
        loads[m].wait()
        keeps[m].start()

    for distance in range(1, nz + 2):
        for m in range(count):
            if distance < nz:
                for d in both(distance):
                    way = 1 if d > 0 else -1

                    def from_z():
                        for t in range(2):
                            z_arrival(m, d, t).wait_recv()
                            if distance < nz - 1:
                                when(ahead(way), lambda: z_copy(m, d, t, way).start())
                            if t == 0:
                                y_copy(m, d).start()
                        c_copy(m, 0, d).start()

                    when(valid(d), from_z)
            if distance - 1 < nz:
                for d in both(distance - 1):

                    def from_y():
                        y_arrival(m, d).wait_recv()
                        x_copy(m, d).start()

                    when(valid(d), from_y)
            if 0 <= distance - 2 < nz:
                for d in both(distance - 2):

                    def from_x():
                        x_arrival(m, d).wait_recv()
                        c_copy(m, 1, d).start()

                    when(valid(d), from_x)

    for m in range(count):
        keeps[m].wait()
        for distance in range(nz):
            for d in both(distance):

                def finish():
                    y_copy(m, d).wait_send()
                    x_copy(m, d).wait_send()
                    for column in range(2):
                        c_copy(m, column, d).wait_send()
                        c_arrival(m, column, d).wait_recv()
                    for way in (1, -1):
                        if d * way >= 0 and distance < nz - 1:
                            for t in range(2):
                                when(ahead(way), lambda: z_copy(m, d, t, way).wait_send())

                when(valid(d), finish)


def gather_kernels(pieces, collective_id):
    devices = lax.axis_size("row")
    nz = devices // 4
    count = len(pieces)
    flat = [p.reshape(-1, p.shape[2], p.shape[3]) for p in pieces]
    taps, rows, out_channels = flat[0].shape
    slots = 2 * nz - 1
    dma = pltpu.SemaphoreType.DMA
    anywhere = pl.BlockSpec(memory_space=pl.ANY)
    outs = pl.pallas_call(
        functools.partial(gather_body, count, nz),
        in_specs=[anywhere] * count,
        out_specs=[anywhere] * count,
        out_shape=[jax.ShapeDtypeStruct((taps, rows * devices, out_channels), BF16)] * count,
        scratch_shapes=[pltpu.VMEM((taps, rows, out_channels), BF16)] * count
        + [dma((count,))] * 2
        + [dma((count, slots, 2))] * 2
        + [dma((count, slots))] * 4
        + [dma((count, 2, slots))] * 2,
        compiler_params=pltpu.CompilerParams(
            collective_id=collective_id, has_side_effects=True, vmem_limit_bytes=16 << 20
        ),
        name="gather_kernels",
    )(*flat)
    return [o.reshape(3, 3, rows * devices, out_channels) for o in outs]


def edge_rows(value):
    size = lax.axis_size("row")
    up = [(i, i + 1) for i in range(size - 1)]
    down = [(j, i) for i, j in up]
    before = lax.ppermute(value[-1:], "row", up)
    after = lax.ppermute(value[:1], "row", down)
    return before, after


def convolve(padded, kernel, out_rows, out_cols):
    total = 0.0
    for u in range(3):
        for v in range(3):
            taps = padded[u : u + out_rows, v : v + out_cols]
            total = total + dot(taps.reshape(-1, taps.shape[2]), kernel[u, v])
    return total


def central_by_rows(latent_out, devices):
    grid_rows, grid_cols, channels = latent_out.shape
    central = latent_out[:, grid_cols // 4 : 3 * grid_cols // 4]
    central_cols = central.shape[1]
    slice_cols = central_cols // devices
    padded = jnp.pad(central, ((0, 0), (1, 1), (0, 0)))
    left = padded[:, :central_cols].reshape(grid_rows, devices, slice_cols, channels)
    first = padded[:, slice_cols::slice_cols]
    second = padded[:, slice_cols + 1 :: slice_cols]
    outgoing = jnp.concatenate([left, first[:, :, None], second[:, :, None]], axis=2)
    arrived = lax.all_to_all(outgoing, "row", split_axis=1, concat_axis=0, tiled=True)
    total_rows = arrived.shape[0]
    return arrived[total_rows // 4 : 3 * total_rows // 4, 0]


def central_by_windows(windows):
    grid_cells, bands, others, channels = windows.shape
    low, high = grid_cells // 4, 3 * grid_cells // 4
    mine = lax.axis_index("row")
    central = windows[low:high, :, others // 4 : 3 * others // 4]
    rows = (high - low) * bands
    central = central.reshape(rows, -1, channels).transpose(1, 0, 2)
    blank = jnp.zeros_like(central[:1])
    even = jnp.where(mine == grid_cells - 1, jnp.concatenate([blank, central[:-1]]), central)
    odd = jnp.where(mine == 0, jnp.concatenate([central[1:], blank]), central)
    outgoing = jnp.stack([even, odd], axis=1).reshape(-1, rows, channels)
    width = bands * others
    both = jnp.concatenate([windows.reshape(grid_cells, width, channels), outgoing], axis=1)
    both = lax.all_to_all(both, "row", split_axis=0, concat_axis=0, tiled=True)
    returned, arrived = both[:, :width].reshape(windows.shape), both[:, width:]
    half = grid_cells // 2
    if_even = jnp.concatenate([arrived[-1:], arrived[: half + 1]])
    if_odd = jnp.concatenate([arrived[half - 1 :], arrived[:1]])
    return returned, jnp.where(mine % 2 == 0, if_even, if_odd).transpose(1, 0, 2)


def on_device(
    latent, conv_first, conv_second, w_query, w_key, w_value, w_out, w_in, w_down, conv_up
):
    devices = lax.axis_size("row")
    grid_rows, grid_cols, channels = latent.shape
    paired = devices % 4 == 0 and lax.axis_size("parts") % 2 == 0
    if paired and devices <= GRID and conv_first.shape[2] % 32 == 0:
        kernels = gather_kernels([conv_first, conv_second], 0)
    else:
        kernels = [whole_kernel(conv_first), whole_kernel(conv_second)]
    up_kernel = whole_kernel(conv_up)
    current = latent
    for kernel in kernels:
        before, after = edge_rows(current)
        current = conv_block(before, current, after, kernel, current)

    step = devices // GRID
    groups = None
    if step > 1:
        groups = [[j + step * c for c in range(GRID)] for j in range(step)]
    exchange = functools.partial(
        lax.all_to_all,
        axis_name="row",
        split_axis=0,
        concat_axis=0,
        tiled=True,
        axis_index_groups=groups,
    )
    by_column = current.reshape(grid_rows, -1, GRID, channels).transpose(2, 0, 1, 3)
    windows = window_block(
        exchange(by_column), w_query, w_key, w_value, w_out, w_in, w_down
    )
    fast = step == 1 and grid_cols == GRID * GRID and channels % 128 == 0
    if fast:
        returned, framed = central_by_windows(windows)
    else:
        returned = exchange(windows)
    latent_out = returned.transpose(1, 2, 0, 3).reshape(grid_rows, grid_cols, channels)
    if not fast:
        framed = central_by_rows(latent_out, devices)
    cols = framed.shape[1] - 2
    doubled = jnp.repeat(framed, 2, axis=1)[:, 1:-1]
    if fast:
        taps = jnp.stack([doubled[:, v : v + 2 * cols] for v in range(3)])
        return latent_out, up_block(taps, up_kernel)
    doubled = jnp.pad(jnp.repeat(doubled, 2, axis=0), ((1, 1), (0, 0), (0, 0)))
    total_rows = doubled.shape[0] - 2
    upsampled = convolve(doubled, up_kernel, total_rows, 2 * cols).astype(BF16)
    return latent_out, upsampled.reshape(total_rows, 2 * cols, channels)


def solution(mesh):
    placed = (
        P(("parts", "row"), None, None),
        P(None, None, "row", None),
        P(None, None, "row", None),
        P(),
        P(),
        P(),
        P(),
        P(),
        P(),
        P(None, None, "row", None),
    )
    return jax.shard_map(
        on_device,
        mesh=mesh,
        in_specs=placed,
        out_specs=(P(("parts", "row"), None, None), P("parts", "row", None)),
        check_vma=False,
    )
```

```python
import functools

import jax
import jax.numpy as jnp
from jax import lax
from jax.experimental import pallas as pl
from jax.experimental.pallas import tpu as pltpu
from jax.sharding import PartitionSpec as P

HD = 64
GRID = 16
F32 = jnp.float32
BF16 = jnp.bfloat16


def gelu(values):
    return jax.nn.gelu(values.astype(F32)).astype(BF16)


def rms_round(values):
    meansq = jnp.mean(values * values, axis=-1, keepdims=True)
    return (values * lax.rsqrt(meansq + 1e-06)).astype(BF16)


def dot(a, b):
    return jnp.dot(a, b, preferred_element_type=F32)


def conv_body(rows, masked, top_ref, mid_ref, bot_ref, k_ref, res_ref, o_ref, act_ref):
    @pl.when(pl.program_id(0) == 0)
    def _():
        act_ref[0] = gelu(top_ref[0])
        for i in range(rows):
            act_ref[i + 1] = gelu(mid_ref[i])
        act_ref[rows + 1] = gelu(bot_ref[0])
        if masked:
            blank = jnp.zeros(act_ref.shape[1:], BF16)

            @pl.when(lax.axis_index("row") == 0)
            def _():
                act_ref[0] = blank

            @pl.when(lax.axis_index("row") == lax.axis_size("row") - 1)
            def _():
                act_ref[rows + 1] = blank

    cols = act_ref.shape[1]
    width = k_ref.shape[3]
    col = lax.broadcasted_iota(jnp.int32, (cols, width), 0)
    for i in range(rows):
        sums = []
        for v in range(3):
            s = dot(act_ref[i], k_ref[0, v])
            s = s + dot(act_ref[i + 1], k_ref[1, v])
            s = s + dot(act_ref[i + 2], k_ref[2, v])
            sums.append(s)
        left = jnp.where(col == 0, 0.0, pltpu.roll(sums[0], 1, 0))
        right = jnp.where(col == cols - 1, 0.0, pltpu.roll(sums[2], cols - 1, 0))
        total = sums[1] + left + right
        o_ref[i] = (res_ref[i].astype(F32) + total).astype(BF16)


def conv_block(top, mid, bot, kernel, residual, masked=False):
    rows, cols, channels = mid.shape
    out_channels = kernel.shape[3]
    width = min(256, out_channels)
    whole = lambda n: pl.BlockSpec((n, cols, channels), lambda b: (0, 0, 0))
    part = pl.BlockSpec((rows, cols, width), lambda b: (0, 0, b))
    return pl.pallas_call(
        functools.partial(conv_body, rows, masked),
        grid=(out_channels // width,),
        in_specs=[
            whole(1),
            whole(rows),
            whole(1),
            pl.BlockSpec((3, 3, channels, width), lambda b: (0, 0, 0, b)),
            part,
        ],
        out_specs=part,
        out_shape=jax.ShapeDtypeStruct((rows, cols, out_channels), BF16),
        scratch_shapes=[pltpu.VMEM((rows + 2, cols, channels), BF16)],
        compiler_params=pltpu.CompilerParams(vmem_limit_bytes=60 * 1024 * 1024),
        name="conv_block",
        cost_estimate=pl.CostEstimate(
            flops=18 * rows * cols * channels * out_channels,
            bytes_accessed=18 * channels * out_channels,
            transcendentals=0,
        ),
    )(top, mid, bot, kernel, residual)


def window_body(x_ref, wq_ref, wk_ref, wv_ref, wo_ref, wi_ref, wd_ref, o_ref, att_ref):
    shape = x_ref.shape
    channels = shape[-1]
    cells = shape[0] * shape[2]
    x = x_ref[:, 0].reshape(cells, channels).astype(F32)
    normed = rms_round(x)
    queries = dot(normed, wq_ref[...]).astype(BF16)
    keys = dot(normed, wk_ref[...]).astype(BF16)
    values = dot(normed, wv_ref[...]).astype(BF16)
    pair = 2 * HD
    lane = lax.broadcasted_iota(jnp.int32, (cells, pair), 1)
    zero = jnp.zeros((cells, pair), BF16)
    for p in range(channels // pair):
        q = queries[:, p * pair : (p + 1) * pair]
        k = keys[:, p * pair : (p + 1) * pair]
        v = values[:, p * pair : (p + 1) * pair]
        out = None
        for half in range(2):
            own = (lane < HD) if half == 0 else (lane >= HD)
            scores = lax.dot_general(
                jnp.where(own, q, zero), k, (((1,), (1,)), ((), ())), preferred_element_type=F32
            ) * HD ** (-0.5)
            lifted = jnp.exp(scores - jnp.max(scores, axis=-1, keepdims=True))
            probs = (lifted * (1.0 / jnp.sum(lifted, axis=-1, keepdims=True))).astype(BF16)
            term = dot(probs, jnp.where(own, v, zero))
            out = term if out is None else out + term
        att_ref[:, p * pair : (p + 1) * pair] = out.astype(BF16)
    y3 = (x + dot(att_ref[...], wo_ref[...])).astype(BF16).astype(F32)
    hidden = gelu(dot(rms_round(y3), wi_ref[...]))
    result = (y3 + dot(hidden, wd_ref[...])).astype(BF16)
    o_ref[:, 0] = result.reshape(shape[0], shape[2], channels)


def window_block(x, *weights):
    grid_cells, bands, others, channels = x.shape
    part = pl.BlockSpec((grid_cells, 1, others, channels), lambda b: (0, b, 0, 0))
    whole = [pl.BlockSpec(w.shape, lambda b: (0, 0), pipeline_mode=pl.Buffered(1)) for w in weights]
    cells = grid_cells * others
    work = sum(w.size for w in weights)
    return pl.pallas_call(
        window_body,
        grid=(bands,),
        in_specs=[part] + whole,
        out_specs=part,
        out_shape=jax.ShapeDtypeStruct(x.shape, BF16),
        scratch_shapes=[pltpu.VMEM((cells, channels), BF16)],
        compiler_params=pltpu.CompilerParams(vmem_limit_bytes=60 * 1024 * 1024),
        name="window_block",
        cost_estimate=pl.CostEstimate(
            flops=2 * bands * cells * (work + 2 * cells * channels),
            bytes_accessed=2 * work,
            transcendentals=bands * cells * (cells * channels // HD),
        ),
    )(x, *weights)


def up_body(d_ref, k_ref, o_ref):
    _, rows, cols, channels = d_ref.shape
    width = k_ref.shape[3]
    sums = []
    for u in range(3):
        s = None
        for v in range(3):
            term = dot(d_ref[v].reshape(rows * cols, channels), k_ref[u, v])
            s = term if s is None else s + term
        sums.append(s.reshape(rows, cols, width))
    for i in range(rows):
        even = sums[1][i] + sums[2][i]
        if i > 0:
            even = even + sums[0][i - 1]
        odd = sums[0][i] + sums[1][i]
        if i < rows - 1:
            odd = odd + sums[2][i + 1]
        o_ref[2 * i] = even.astype(BF16)
        o_ref[2 * i + 1] = odd.astype(BF16)


def up_block(doubled, kernel):
    _, rows, cols, channels = doubled.shape
    out_channels = kernel.shape[3]
    width = min(256, out_channels)
    return pl.pallas_call(
        up_body,
        grid=(out_channels // width,),
        in_specs=[
            pl.BlockSpec(doubled.shape, lambda b: (0, 0, 0, 0)),
            pl.BlockSpec((3, 3, channels, width), lambda b: (0, 0, 0, b)),
        ],
        out_specs=pl.BlockSpec((2 * rows, cols, width), lambda b: (0, 0, b)),
        out_shape=jax.ShapeDtypeStruct((2 * rows, cols, out_channels), BF16),
        compiler_params=pltpu.CompilerParams(vmem_limit_bytes=60 * 1024 * 1024),
        name="up_block",
        cost_estimate=pl.CostEstimate(
            flops=18 * rows * cols * channels * out_channels,
            bytes_accessed=18 * channels * out_channels,
            transcendentals=0,
        ),
    )(doubled, kernel)


def whole_kernel(kernel_piece):
    return lax.all_gather(kernel_piece, "row", axis=2, tiled=True)


def gather_body(count, nz, *refs):
    pieces, field = refs[:count], refs[count]
    wholes, before, after = refs[count + 1 : 2 * count + 1], refs[2 * count + 1], refs[2 * count + 2]
    owns = refs[2 * count + 3 : 3 * count + 3]
    load_sem, keep_sem, zs, zr, ys, yr, xs, xr, cs, cr, es, er = refs[3 * count + 3 :]
    index, part = lax.axis_index("row"), lax.axis_index("parts")
    core, y, z = index % 2, (index // 2) % 2, index // 4
    parity = part % 2
    taps, rows, _ = pieces[0].shape
    half = rows // 2
    zero = nz - 1

    def device(z_, y_, core_, part_):
        return {"parts": part_, "row": (z_ * 2 + y_) * 2 + core_}

    def place(ref, z_, y_, t):
        base = ((z_ * 2 + y_) * 2 + core) * rows
        size = rows
        if t is not None:
            base = base + ((parity + t) % 2) * half
            size = half
        return ref.at[:, pl.ds(pl.multiple_of(base, size), size)]

    def source(m, d, t):
        if d != 0:
            return place(wholes[m], z - d, y, t)
        if t is None:
            return pieces[m]
        return pieces[m].at[:, pl.ds(pl.multiple_of(((parity + t) % 2) * half, half), half)]

    def remote(src, dst, send, recv, to):
        return pltpu.make_async_remote_copy(
            src_ref=src,
            dst_ref=dst,
            send_sem=send,
            recv_sem=recv,
            device_id=to,
            device_id_type=pl.DeviceIdType.MESH,
        )

    def z_copy(m, d, t, way):
        slot = d + way + zero
        return remote(
            source(m, d, t),
            place(wholes[m], z - d, y, t),
            zs.at[m, slot, t],
            zr.at[m, slot, t],
            device(z + way, y, core, part),
        )

    def z_arrival(m, d, t):
        here = place(wholes[m], z - d, y, t)
        way = 1 if d > 0 else -1
        slot = d + zero
        return remote(
            here, here, zs.at[m, slot, t], zr.at[m, slot, t], device(z - way, y, core, part)
        )

    def y_copy(m, d):
        slot = d + zero
        return remote(
            source(m, d, 0),
            place(wholes[m], z - d, y, 0),
            ys.at[m, slot],
            yr.at[m, slot],
            device(z, 1 - y, core, part),
        )

    def y_arrival(m, d):
        here = place(wholes[m], z - d, 1 - y, 0)
        slot = d + zero
        return remote(here, here, ys.at[m, slot], yr.at[m, slot], device(z, 1 - y, core, part))

    def x_copy(m, d):
        here = place(wholes[m], z - d, 1 - y, 0)
        slot = d + zero
        to = device(z, y, core, part + 1 - 2 * parity)
        return remote(here, here, xs.at[m, slot], xr.at[m, slot], to)

    def x_arrival(m, d):
        here = place(wholes[m], z - d, 1 - y, 1)
        slot = d + zero
        to = device(z, y, core, part + 1 - 2 * parity)
        return remote(here, here, xs.at[m, slot], xr.at[m, slot], to)

    def c_copy(m, column, d):
        slot = d + zero
        to = device(z, y, 1 - core, part)
        if column == 0:
            src, dst = source(m, d, None), place(wholes[m], z - d, y, None)
        else:
            src = place(wholes[m], z - d, 1 - y, None)
            dst = src
        return remote(src, dst, cs.at[m, column, slot], cr.at[m, column, slot], to)

    def c_arrival(m, column, d):
        slot = d + zero
        y_ = y if column == 0 else 1 - y
        base = ((z - d) * 2 + y_) * 2 + 1 - core
        here = wholes[m].at[:, pl.ds(pl.multiple_of(base * rows, rows), rows)]
        to = device(z, y, 1 - core, part)
        return remote(here, here, cs.at[m, column, slot], cr.at[m, column, slot], to)

    def edge(way):
        src = field.at[pl.ds(field.shape[0] - 1 if way > 0 else 0, 1)]
        dst = before if way > 0 else after
        slot = 0 if way > 0 else 1
        return remote(src, dst, es.at[slot], er.at[slot], {"parts": part, "row": index + way})

    def edge_arrival(way):
        dst = before if way > 0 else after
        slot = 0 if way > 0 else 1
        return remote(dst, dst, es.at[slot], er.at[slot], {"parts": part, "row": index - way})

    def beside(way):
        return index < 4 * nz - 1 if way > 0 else index > 0

    def when(condition, action):
        if condition is None:
            action()
        else:
            pl.when(condition)(action)

    def valid(d):
        if d == 0:
            return None
        return z >= d if d > 0 else z - d <= nz - 1

    def ahead(way):
        return z < nz - 1 if way > 0 else z > 0

    def both(distance):
        return (0,) if distance == 0 else (distance, -distance)

    barrier = pltpu.get_barrier_semaphore()

    def greet(to):
        pl.semaphore_signal(
            barrier, inc=1, device_id=to, device_id_type=pl.DeviceIdType.MESH
        )

    greet(device(z, 1 - y, core, part))
    greet(device(z, y, 1 - core, part))
    greet(device(z, y, core, part + 1 - 2 * parity))
    for way in (1, -1):
        when(ahead(way), functools.partial(greet, device(z + way, y, core, part)))
        when(beside(way), functools.partial(greet, {"parts": part, "row": index + way}))
    peers = 3 + jnp.minimum(z, 1) + jnp.minimum(nz - 1 - z, 1)
    peers = peers + jnp.minimum(index, 1) + jnp.minimum(4 * nz - 1 - index, 1)
    pl.semaphore_wait(barrier, peers)

    loads = [
        pltpu.make_async_copy(pieces[m], owns[m], load_sem.at[m]) for m in range(count)
    ]
    keeps = [
        pltpu.make_async_copy(owns[m], place(wholes[m], z, y, None), keep_sem.at[m])
        for m in range(count)
    ]
    for m in range(count):
        for t in range(2):
            for way in (1, -1):
                when(ahead(way), lambda: z_copy(m, 0, t, way).start())
        y_copy(m, 0).start()
        c_copy(m, 0, 0).start()
        loads[m].start()
    for way in (1, -1):
        when(beside(way), lambda: edge(way).start())
    for m in range(count):
        loads[m].wait()
        keeps[m].start()

    for distance in range(1, nz + 2):
        for m in range(count):
            if distance < nz:
                for d in both(distance):
                    way = 1 if d > 0 else -1

                    def from_z():
                        for t in range(2):
                            z_arrival(m, d, t).wait_recv()
                            if distance < nz - 1:
                                when(ahead(way), lambda: z_copy(m, d, t, way).start())
                            if t == 0:
                                y_copy(m, d).start()
                        c_copy(m, 0, d).start()

                    when(valid(d), from_z)
            if distance - 1 < nz:
                for d in both(distance - 1):

                    def from_y():
                        y_arrival(m, d).wait_recv()
                        x_copy(m, d).start()

                    when(valid(d), from_y)
            if 0 <= distance - 2 < nz:
                for d in both(distance - 2):

                    def from_x():
                        x_arrival(m, d).wait_recv()
                        c_copy(m, 1, d).start()

                    when(valid(d), from_x)

    for way in (1, -1):
        when(beside(way), lambda: edge(way).wait_send())
        when(beside(-way), lambda: edge_arrival(way).wait_recv())
    for m in range(count):
        keeps[m].wait()
        for distance in range(nz):
            for d in both(distance):

                def finish():
                    y_copy(m, d).wait_send()
                    x_copy(m, d).wait_send()
                    for column in range(2):
                        c_copy(m, column, d).wait_send()
                        c_arrival(m, column, d).wait_recv()
                    for way in (1, -1):
                        if d * way >= 0 and distance < nz - 1:
                            for t in range(2):
                                when(ahead(way), lambda: z_copy(m, d, t, way).wait_send())

                when(valid(d), finish)


def gather_kernels(pieces, field, collective_id):
    devices = lax.axis_size("row")
    nz = devices // 4
    count = len(pieces)
    flat = [p.reshape(-1, p.shape[2], p.shape[3]) for p in pieces]
    taps, rows, out_channels = flat[0].shape
    slots = 2 * nz - 1
    dma = pltpu.SemaphoreType.DMA
    anywhere = pl.BlockSpec(memory_space=pl.ANY)
    outs = pl.pallas_call(
        functools.partial(gather_body, count, nz),
        in_specs=[anywhere] * (count + 1),
        out_specs=[anywhere] * (count + 2),
        out_shape=[jax.ShapeDtypeStruct((taps, rows * devices, out_channels), BF16)] * count
        + [jax.ShapeDtypeStruct((1,) + field.shape[1:], BF16)] * 2,
        scratch_shapes=[pltpu.VMEM((taps, rows, out_channels), BF16)] * count
        + [dma((count,))] * 2
        + [dma((count, slots, 2))] * 2
        + [dma((count, slots))] * 4
        + [dma((count, 2, slots))] * 2
        + [dma((2,))] * 2,
        compiler_params=pltpu.CompilerParams(
            collective_id=collective_id, has_side_effects=True, vmem_limit_bytes=60 * 1024 * 1024
        ),
        name="gather_kernels",
    )(*flat, field)
    wholes = [o.reshape(3, 3, rows * devices, out_channels) for o in outs[:count]]
    return wholes, outs[count:]


def edge_rows(value):
    size = lax.axis_size("row")
    up = [(i, i + 1) for i in range(size - 1)]
    down = [(j, i) for i, j in up]
    before = lax.ppermute(value[-1:], "row", up)
    after = lax.ppermute(value[:1], "row", down)
    return before, after


def convolve(padded, kernel, out_rows, out_cols):
    total = 0.0
    for u in range(3):
        for v in range(3):
            taps = padded[u : u + out_rows, v : v + out_cols]
            total = total + dot(taps.reshape(-1, taps.shape[2]), kernel[u, v])
    return total


def central_by_rows(latent_out, devices):
    grid_rows, grid_cols, channels = latent_out.shape
    central = latent_out[:, grid_cols // 4 : 3 * grid_cols // 4]
    central_cols = central.shape[1]
    slice_cols = central_cols // devices
    padded = jnp.pad(central, ((0, 0), (1, 1), (0, 0)))
    left = padded[:, :central_cols].reshape(grid_rows, devices, slice_cols, channels)
    first = padded[:, slice_cols::slice_cols]
    second = padded[:, slice_cols + 1 :: slice_cols]
    outgoing = jnp.concatenate([left, first[:, :, None], second[:, :, None]], axis=2)
    arrived = lax.all_to_all(outgoing, "row", split_axis=1, concat_axis=0, tiled=True)
    total_rows = arrived.shape[0]
    return arrived[total_rows // 4 : 3 * total_rows // 4, 0]


def central_by_windows(windows):
    grid_cells, bands, others, channels = windows.shape
    low, high = grid_cells // 4, 3 * grid_cells // 4
    mine = lax.axis_index("row")
    central = windows[low:high, :, others // 4 : 3 * others // 4]
    rows = (high - low) * bands
    central = central.reshape(rows, -1, channels).transpose(1, 0, 2)
    blank = jnp.zeros_like(central[:1])
    even = jnp.where(mine == grid_cells - 1, jnp.concatenate([blank, central[:-1]]), central)
    odd = jnp.where(mine == 0, jnp.concatenate([central[1:], blank]), central)
    outgoing = jnp.stack([even, odd], axis=1).reshape(-1, rows, channels)
    width = bands * others
    both = jnp.concatenate([windows.reshape(grid_cells, width, channels), outgoing], axis=1)
    both = lax.all_to_all(both, "row", split_axis=0, concat_axis=0, tiled=True)
    returned, arrived = both[:, :width].reshape(windows.shape), both[:, width:]
    half = grid_cells // 2
    if_even = jnp.concatenate([arrived[-1:], arrived[: half + 1]])
    if_odd = jnp.concatenate([arrived[half - 1 :], arrived[:1]])
    return returned, jnp.where(mine % 2 == 0, if_even, if_odd).transpose(1, 0, 2)


def on_device(
    latent, conv_first, conv_second, w_query, w_key, w_value, w_out, w_in, w_down, conv_up
):
    devices = lax.axis_size("row")
    grid_rows, grid_cols, channels = latent.shape
    paired = devices % 4 == 0 and lax.axis_size("parts") % 2 == 0
    if paired and devices <= GRID and conv_first.shape[2] % 32 == 0:
        kernels, edges = gather_kernels([conv_first, conv_second, conv_up], latent, 0)
        first, second, up_kernel = kernels
        current = conv_block(edges[0], latent, edges[1], first, latent, True)
    else:
        first, second, up_kernel = [whole_kernel(k) for k in (conv_first, conv_second, conv_up)]
        before, after = edge_rows(latent)
        current = conv_block(before, latent, after, first, latent)
    before, after = edge_rows(current)
    current = conv_block(before, current, after, second, current)

    step = devices // GRID
    groups = None
    if step > 1:
        groups = [[j + step * c for c in range(GRID)] for j in range(step)]
    exchange = functools.partial(
        lax.all_to_all,
        axis_name="row",
        split_axis=0,
        concat_axis=0,
        tiled=True,
        axis_index_groups=groups,
    )
    by_column = current.reshape(grid_rows, -1, GRID, channels).transpose(2, 0, 1, 3)
    windows = window_block(
        exchange(by_column), w_query, w_key, w_value, w_out, w_in, w_down
    )
    fast = step == 1 and grid_cols == GRID * GRID and channels % 128 == 0
    if fast:
        returned, framed = central_by_windows(windows)
    else:
        returned = exchange(windows)
    latent_out = returned.transpose(1, 2, 0, 3).reshape(grid_rows, grid_cols, channels)
    if not fast:
        framed = central_by_rows(latent_out, devices)
    cols = framed.shape[1] - 2
    doubled = jnp.repeat(framed, 2, axis=1)[:, 1:-1]
    if fast:
        taps = jnp.stack([doubled[:, v : v + 2 * cols] for v in range(3)])
        return latent_out, up_block(taps, up_kernel)
    doubled = jnp.pad(jnp.repeat(doubled, 2, axis=0), ((1, 1), (0, 0), (0, 0)))
    total_rows = doubled.shape[0] - 2
    upsampled = convolve(doubled, up_kernel, total_rows, 2 * cols).astype(BF16)
    return latent_out, upsampled.reshape(total_rows, 2 * cols, channels)


def solution(mesh):
    placed = (
        P(("parts", "row"), None, None),
        P(None, None, "row", None),
        P(None, None, "row", None),
        P(),
        P(),
        P(),
        P(),
        P(),
        P(),
        P(None, None, "row", None),
    )
    return jax.shard_map(
        on_device,
        mesh=mesh,
        in_specs=placed,
        out_specs=(P(("parts", "row"), None, None), P("parts", "row", None)),
        check_vma=False,
    )
```

```python
import functools

import jax
import jax.numpy as jnp
from jax import lax
from jax.experimental import pallas as pl
from jax.experimental.pallas import tpu as pltpu
from jax.sharding import PartitionSpec as P

HD = 64
GRID = 16
F32 = jnp.float32
BF16 = jnp.bfloat16


def gelu(values):
    return jax.nn.gelu(values.astype(F32)).astype(BF16)


def rms_round(values):
    meansq = jnp.mean(values * values, axis=-1, keepdims=True)
    return (values * lax.rsqrt(meansq + 1e-06)).astype(BF16)


def dot(a, b):
    return jnp.dot(a, b, preferred_element_type=F32)


def conv_body(rows, masked, top_ref, mid_ref, bot_ref, k_ref, res_ref, o_ref, act_ref):
    @pl.when(pl.program_id(0) == 0)
    def _():
        act_ref[0] = gelu(top_ref[0])
        for i in range(rows):
            act_ref[i + 1] = gelu(mid_ref[i])
        act_ref[rows + 1] = gelu(bot_ref[0])
        if masked:
            blank = jnp.zeros(act_ref.shape[1:], BF16)

            @pl.when(lax.axis_index("row") == 0)
            def _():
                act_ref[0] = blank

            @pl.when(lax.axis_index("row") == lax.axis_size("row") - 1)
            def _():
                act_ref[rows + 1] = blank

    cols = act_ref.shape[1]
    width = k_ref.shape[3]
    col = lax.broadcasted_iota(jnp.int32, (cols, width), 0)
    for i in range(rows):
        sums = []
        for v in range(3):
            s = dot(act_ref[i], k_ref[0, v])
            s = s + dot(act_ref[i + 1], k_ref[1, v])
            s = s + dot(act_ref[i + 2], k_ref[2, v])
            sums.append(s)
        left = jnp.where(col == 0, 0.0, pltpu.roll(sums[0], 1, 0))
        right = jnp.where(col == cols - 1, 0.0, pltpu.roll(sums[2], cols - 1, 0))
        total = sums[1] + left + right
        o_ref[i] = (res_ref[i].astype(F32) + total).astype(BF16)


def conv_block(top, mid, bot, kernel, residual, masked=False):
    rows, cols, channels = mid.shape
    out_channels = kernel.shape[3]
    width = min(256, out_channels)
    whole = lambda n: pl.BlockSpec((n, cols, channels), lambda b: (0, 0, 0))
    part = pl.BlockSpec((rows, cols, width), lambda b: (0, 0, b))
    return pl.pallas_call(
        functools.partial(conv_body, rows, masked),
        grid=(out_channels // width,),
        in_specs=[
            whole(1),
            whole(rows),
            whole(1),
            pl.BlockSpec((3, 3, channels, width), lambda b: (0, 0, 0, b)),
            part,
        ],
        out_specs=part,
        out_shape=jax.ShapeDtypeStruct((rows, cols, out_channels), BF16),
        scratch_shapes=[pltpu.VMEM((rows + 2, cols, channels), BF16)],
        compiler_params=pltpu.CompilerParams(vmem_limit_bytes=60 * 1024 * 1024),
        name="conv_block",
        cost_estimate=pl.CostEstimate(
            flops=18 * rows * cols * channels * out_channels,
            bytes_accessed=18 * channels * out_channels,
            transcendentals=0,
        ),
    )(top, mid, bot, kernel, residual)


def window_body(x_ref, wq_ref, wk_ref, wv_ref, wo_ref, wi_ref, wd_ref, o_ref, att_ref):
    shape = x_ref.shape
    channels = shape[-1]
    cells = shape[0] * shape[2]
    x = x_ref[:, 0].reshape(cells, channels).astype(F32)
    normed = rms_round(x)
    queries = dot(normed, wq_ref[...]).astype(BF16)
    keys = dot(normed, wk_ref[...]).astype(BF16)
    values = dot(normed, wv_ref[...]).astype(BF16)
    pair = 2 * HD
    lane = lax.broadcasted_iota(jnp.int32, (cells, pair), 1)
    zero = jnp.zeros((cells, pair), BF16)
    for p in range(channels // pair):
        q = queries[:, p * pair : (p + 1) * pair]
        k = keys[:, p * pair : (p + 1) * pair]
        v = values[:, p * pair : (p + 1) * pair]
        out = None
        for half in range(2):
            own = (lane < HD) if half == 0 else (lane >= HD)
            scores = lax.dot_general(
                jnp.where(own, q, zero), k, (((1,), (1,)), ((), ())), preferred_element_type=F32
            ) * HD ** (-0.5)
            lifted = jnp.exp(scores - jnp.max(scores, axis=-1, keepdims=True))
            probs = (lifted * (1.0 / jnp.sum(lifted, axis=-1, keepdims=True))).astype(BF16)
            term = dot(probs, jnp.where(own, v, zero))
            out = term if out is None else out + term
        att_ref[:, p * pair : (p + 1) * pair] = out.astype(BF16)
    y3 = (x + dot(att_ref[...], wo_ref[...])).astype(BF16).astype(F32)
    hidden = gelu(dot(rms_round(y3), wi_ref[...]))
    result = (y3 + dot(hidden, wd_ref[...])).astype(BF16)
    o_ref[:, 0] = result.reshape(shape[0], shape[2], channels)


def window_block(x, *weights):
    grid_cells, bands, others, channels = x.shape
    part = pl.BlockSpec((grid_cells, 1, others, channels), lambda b: (0, b, 0, 0))
    whole = [pl.BlockSpec(w.shape, lambda b: (0, 0), pipeline_mode=pl.Buffered(1)) for w in weights]
    cells = grid_cells * others
    work = sum(w.size for w in weights)
    return pl.pallas_call(
        window_body,
        grid=(bands,),
        in_specs=[part] + whole,
        out_specs=part,
        out_shape=jax.ShapeDtypeStruct(x.shape, BF16),
        scratch_shapes=[pltpu.VMEM((cells, channels), BF16)],
        compiler_params=pltpu.CompilerParams(vmem_limit_bytes=60 * 1024 * 1024),
        name="window_block",
        cost_estimate=pl.CostEstimate(
            flops=2 * bands * cells * (work + 2 * cells * channels),
            bytes_accessed=2 * work,
            transcendentals=bands * cells * (cells * channels // HD),
        ),
    )(x, *weights)


def up_body(d_ref, k_ref, o_ref):
    _, rows, cols, channels = d_ref.shape
    width = k_ref.shape[3]
    sums = []
    for u in range(3):
        s = None
        for v in range(3):
            term = dot(d_ref[v].reshape(rows * cols, channels), k_ref[u, v])
            s = term if s is None else s + term
        sums.append(s.reshape(rows, cols, width))
    for i in range(rows):
        even = sums[1][i] + sums[2][i]
        if i > 0:
            even = even + sums[0][i - 1]
        odd = sums[0][i] + sums[1][i]
        if i < rows - 1:
            odd = odd + sums[2][i + 1]
        o_ref[2 * i] = even.astype(BF16)
        o_ref[2 * i + 1] = odd.astype(BF16)


def up_block(doubled, kernel):
    _, rows, cols, channels = doubled.shape
    out_channels = kernel.shape[3]
    width = min(256, out_channels)
    return pl.pallas_call(
        up_body,
        grid=(out_channels // width,),
        in_specs=[
            pl.BlockSpec(doubled.shape, lambda b: (0, 0, 0, 0)),
            pl.BlockSpec((3, 3, channels, width), lambda b: (0, 0, 0, b)),
        ],
        out_specs=pl.BlockSpec((2 * rows, cols, width), lambda b: (0, 0, b)),
        out_shape=jax.ShapeDtypeStruct((2 * rows, cols, out_channels), BF16),
        compiler_params=pltpu.CompilerParams(vmem_limit_bytes=60 * 1024 * 1024),
        name="up_block",
        cost_estimate=pl.CostEstimate(
            flops=18 * rows * cols * channels * out_channels,
            bytes_accessed=18 * channels * out_channels,
            transcendentals=0,
        ),
    )(doubled, kernel)


def whole_kernel(kernel_piece):
    return lax.all_gather(kernel_piece, "row", axis=2, tiled=True)


def gather_body(count, nz, *refs):
    pieces, field = refs[:count], refs[count]
    wholes, before, after = refs[count + 1 : 2 * count + 1], refs[2 * count + 1], refs[2 * count + 2]
    owns = refs[2 * count + 3 : 3 * count + 3]
    load_sem, keep_sem, zs, zr, ys, yr, xs, xr, cs, cr, es, er = refs[3 * count + 3 :]
    index, part = lax.axis_index("row"), lax.axis_index("parts")
    core, y, z = index % 2, (index // 2) % 2, index // 4
    parity = part % 2
    taps, rows, _ = pieces[0].shape
    half = rows // 2
    zero = nz - 1

    def device(z_, y_, core_, part_):
        return {"parts": part_, "row": (z_ * 2 + y_) * 2 + core_}

    def place(ref, z_, y_, t):
        base = ((z_ * 2 + y_) * 2 + core) * rows
        size = rows
        if t is not None:
            base = base + ((parity + t) % 2) * half
            size = half
        return ref.at[:, pl.ds(pl.multiple_of(base, size), size)]

    def source(m, d, t):
        if d != 0:
            return place(wholes[m], z - d, y, t)
        if t is None:
            return pieces[m]
        return pieces[m].at[:, pl.ds(pl.multiple_of(((parity + t) % 2) * half, half), half)]

    def remote(src, dst, send, recv, to):
        return pltpu.make_async_remote_copy(
            src_ref=src,
            dst_ref=dst,
            send_sem=send,
            recv_sem=recv,
            device_id=to,
            device_id_type=pl.DeviceIdType.MESH,
        )

    def z_copy(m, d, t, way):
        slot = d + way + zero
        return remote(
            source(m, d, t),
            place(wholes[m], z - d, y, t),
            zs.at[m, slot, t],
            zr.at[m, slot, t],
            device(z + way, y, core, part),
        )

    def z_arrival(m, d, t):
        here = place(wholes[m], z - d, y, t)
        way = 1 if d > 0 else -1
        slot = d + zero
        return remote(
            here, here, zs.at[m, slot, t], zr.at[m, slot, t], device(z - way, y, core, part)
        )

    def y_copy(m, d):
        slot = d + zero
        return remote(
            source(m, d, 0),
            place(wholes[m], z - d, y, 0),
            ys.at[m, slot],
            yr.at[m, slot],
            device(z, 1 - y, core, part),
        )

    def y_arrival(m, d):
        here = place(wholes[m], z - d, 1 - y, 0)
        slot = d + zero
        return remote(here, here, ys.at[m, slot], yr.at[m, slot], device(z, 1 - y, core, part))

    def x_move(m, column, d, t):
        here = place(wholes[m], z - d, y if column == 0 else 1 - y, t)
        slot = d + zero
        to = device(z, y, core, part + 1 - 2 * parity)
        return remote(here, here, xs.at[m, column, slot], xr.at[m, column, slot], to)

    def x_copy(m, d, column=1):
        return x_move(m, column, d, 0)

    def x_arrival(m, d, column=1):
        return x_move(m, column, d, 1)

    def lean(m):
        return m % 3 == 1

    def halves(m):
        return (0,) if lean(m) else (0, 1)

    def c_copy(m, column, d):
        slot = d + zero
        to = device(z, y, 1 - core, part)
        if column == 0:
            src, dst = source(m, d, None), place(wholes[m], z - d, y, None)
        else:
            src = place(wholes[m], z - d, 1 - y, None)
            dst = src
        return remote(src, dst, cs.at[m, column, slot], cr.at[m, column, slot], to)

    def c_arrival(m, column, d):
        slot = d + zero
        y_ = y if column == 0 else 1 - y
        base = ((z - d) * 2 + y_) * 2 + 1 - core
        here = wholes[m].at[:, pl.ds(pl.multiple_of(base * rows, rows), rows)]
        to = device(z, y, 1 - core, part)
        return remote(here, here, cs.at[m, column, slot], cr.at[m, column, slot], to)

    def edge(way):
        src = field.at[pl.ds(field.shape[0] - 1 if way > 0 else 0, 1)]
        dst = before if way > 0 else after
        slot = 0 if way > 0 else 1
        return remote(src, dst, es.at[slot], er.at[slot], {"parts": part, "row": index + way})

    def edge_arrival(way):
        dst = before if way > 0 else after
        slot = 0 if way > 0 else 1
        return remote(dst, dst, es.at[slot], er.at[slot], {"parts": part, "row": index - way})

    def beside(way):
        return index < 4 * nz - 1 if way > 0 else index > 0

    def when(condition, action):
        if condition is None:
            action()
        else:
            pl.when(condition)(action)

    def valid(d):
        if d == 0:
            return None
        return z >= d if d > 0 else z - d <= nz - 1

    def ahead(way):
        return z < nz - 1 if way > 0 else z > 0

    def both(distance):
        return (0,) if distance == 0 else (distance, -distance)

    barrier = pltpu.get_barrier_semaphore()

    def greet(to):
        pl.semaphore_signal(
            barrier, inc=1, device_id=to, device_id_type=pl.DeviceIdType.MESH
        )

    greet(device(z, 1 - y, core, part))
    greet(device(z, y, 1 - core, part))
    greet(device(z, y, core, part + 1 - 2 * parity))
    for way in (1, -1):
        when(ahead(way), functools.partial(greet, device(z + way, y, core, part)))
        when(beside(way), functools.partial(greet, {"parts": part, "row": index + way}))
    peers = 3 + jnp.minimum(z, 1) + jnp.minimum(nz - 1 - z, 1)
    peers = peers + jnp.minimum(index, 1) + jnp.minimum(4 * nz - 1 - index, 1)
    pl.semaphore_wait(barrier, peers)

    loads = [
        pltpu.make_async_copy(pieces[m], owns[m], load_sem.at[m]) for m in range(count)
    ]
    keeps = [
        pltpu.make_async_copy(owns[m], place(wholes[m], z, y, None), keep_sem.at[m])
        for m in range(count)
    ]
    for m in range(count):
        for t in halves(m):
            for way in (1, -1):
                when(ahead(way), lambda: z_copy(m, 0, t, way).start())
        y_copy(m, 0).start()
        c_copy(m, 0, 0).start()
        loads[m].start()
    for way in (1, -1):
        when(beside(way), lambda: edge(way).start())
    for m in range(count):
        loads[m].wait()
        keeps[m].start()

    for distance in range(1, nz + 2):
        for m in range(count):
            if distance < nz:
                for d in both(distance):
                    way = 1 if d > 0 else -1

                    def from_z():
                        for t in halves(m):
                            z_arrival(m, d, t).wait_recv()
                            if distance < nz - 1:
                                when(ahead(way), lambda: z_copy(m, d, t, way).start())
                            if t == 0:
                                y_copy(m, d).start()
                        if lean(m):
                            x_copy(m, d, 0).start()
                        else:
                            c_copy(m, 0, d).start()

                    when(valid(d), from_z)
            if lean(m) and 1 <= distance - 1 < nz:
                for d in both(distance - 1):

                    def from_part():
                        x_arrival(m, d, 0).wait_recv()
                        c_copy(m, 0, d).start()

                    when(valid(d), from_part)
            if distance - 1 < nz:
                for d in both(distance - 1):

                    def from_y():
                        y_arrival(m, d).wait_recv()
                        x_copy(m, d).start()

                    when(valid(d), from_y)
            if 0 <= distance - 2 < nz:
                for d in both(distance - 2):

                    def from_x():
                        x_arrival(m, d).wait_recv()
                        c_copy(m, 1, d).start()

                    when(valid(d), from_x)

    for way in (1, -1):
        when(beside(way), lambda: edge(way).wait_send())
        when(beside(-way), lambda: edge_arrival(way).wait_recv())
    for m in range(count):
        keeps[m].wait()
        for distance in range(nz):
            for d in both(distance):

                def finish():
                    y_copy(m, d).wait_send()
                    x_copy(m, d).wait_send()
                    if lean(m) and distance > 0:
                        x_copy(m, d, 0).wait_send()
                    for column in range(2):
                        c_copy(m, column, d).wait_send()
                        c_arrival(m, column, d).wait_recv()
                    for way in (1, -1):
                        if d * way >= 0 and distance < nz - 1:
                            for t in halves(m):
                                when(ahead(way), lambda: z_copy(m, d, t, way).wait_send())

                when(valid(d), finish)


def gather_kernels(pieces, field, collective_id):
    devices = lax.axis_size("row")
    nz = devices // 4
    count = len(pieces)
    flat = [p.reshape(-1, p.shape[2], p.shape[3]) for p in pieces]
    taps, rows, out_channels = flat[0].shape
    slots = 2 * nz - 1
    dma = pltpu.SemaphoreType.DMA
    anywhere = pl.BlockSpec(memory_space=pl.ANY)
    outs = pl.pallas_call(
        functools.partial(gather_body, count, nz),
        in_specs=[anywhere] * (count + 1),
        out_specs=[anywhere] * (count + 2),
        out_shape=[jax.ShapeDtypeStruct((taps, rows * devices, out_channels), BF16)] * count
        + [jax.ShapeDtypeStruct((1,) + field.shape[1:], BF16)] * 2,
        scratch_shapes=[pltpu.VMEM((taps, rows, out_channels), BF16)] * count
        + [dma((count,))] * 2
        + [dma((count, slots, 2))] * 2
        + [dma((count, slots))] * 2
        + [dma((count, 2, slots))] * 4
        + [dma((2,))] * 2,
        compiler_params=pltpu.CompilerParams(
            collective_id=collective_id, has_side_effects=True, vmem_limit_bytes=60 * 1024 * 1024
        ),
        name="gather_kernels",
    )(*flat, field)
    wholes = [o.reshape(3, 3, rows * devices, out_channels) for o in outs[:count]]
    return wholes, outs[count:]


def edge_rows(value):
    size = lax.axis_size("row")
    up = [(i, i + 1) for i in range(size - 1)]
    down = [(j, i) for i, j in up]
    before = lax.ppermute(value[-1:], "row", up)
    after = lax.ppermute(value[:1], "row", down)
    return before, after


def convolve(padded, kernel, out_rows, out_cols):
    total = 0.0
    for u in range(3):
        for v in range(3):
            taps = padded[u : u + out_rows, v : v + out_cols]
            total = total + dot(taps.reshape(-1, taps.shape[2]), kernel[u, v])
    return total


def central_by_rows(latent_out, devices):
    grid_rows, grid_cols, channels = latent_out.shape
    central = latent_out[:, grid_cols // 4 : 3 * grid_cols // 4]
    central_cols = central.shape[1]
    slice_cols = central_cols // devices
    padded = jnp.pad(central, ((0, 0), (1, 1), (0, 0)))
    left = padded[:, :central_cols].reshape(grid_rows, devices, slice_cols, channels)
    first = padded[:, slice_cols::slice_cols]
    second = padded[:, slice_cols + 1 :: slice_cols]
    outgoing = jnp.concatenate([left, first[:, :, None], second[:, :, None]], axis=2)
    arrived = lax.all_to_all(outgoing, "row", split_axis=1, concat_axis=0, tiled=True)
    total_rows = arrived.shape[0]
    return arrived[total_rows // 4 : 3 * total_rows // 4, 0]


def central_by_windows(windows):
    grid_cells, bands, others, channels = windows.shape
    low, high = grid_cells // 4, 3 * grid_cells // 4
    mine = lax.axis_index("row")
    central = windows[low:high, :, others // 4 : 3 * others // 4]
    rows = (high - low) * bands
    central = central.reshape(rows, -1, channels).transpose(1, 0, 2)
    blank = jnp.zeros_like(central[:1])
    even = jnp.where(mine == grid_cells - 1, jnp.concatenate([blank, central[:-1]]), central)
    odd = jnp.where(mine == 0, jnp.concatenate([central[1:], blank]), central)
    outgoing = jnp.stack([even, odd], axis=1).reshape(-1, rows, channels)
    width = bands * others
    both = jnp.concatenate([windows.reshape(grid_cells, width, channels), outgoing], axis=1)
    both = lax.all_to_all(both, "row", split_axis=0, concat_axis=0, tiled=True)
    returned, arrived = both[:, :width].reshape(windows.shape), both[:, width:]
    half = grid_cells // 2
    if_even = jnp.concatenate([arrived[-1:], arrived[: half + 1]])
    if_odd = jnp.concatenate([arrived[half - 1 :], arrived[:1]])
    return returned, jnp.where(mine % 2 == 0, if_even, if_odd).transpose(1, 0, 2)


def on_device(
    latent, conv_first, conv_second, w_query, w_key, w_value, w_out, w_in, w_down, conv_up
):
    devices = lax.axis_size("row")
    grid_rows, grid_cols, channels = latent.shape
    paired = devices % 4 == 0 and lax.axis_size("parts") % 2 == 0
    if paired and devices <= GRID and conv_first.shape[2] % 32 == 0:
        kernels, edges = gather_kernels([conv_first, conv_second, conv_up], latent, 0)
        first, second, up_kernel = kernels
        current = conv_block(edges[0], latent, edges[1], first, latent, True)
    else:
        first, second, up_kernel = [whole_kernel(k) for k in (conv_first, conv_second, conv_up)]
        before, after = edge_rows(latent)
        current = conv_block(before, latent, after, first, latent)
    before, after = edge_rows(current)
    current = conv_block(before, current, after, second, current)

    step = devices // GRID
    groups = None
    if step > 1:
        groups = [[j + step * c for c in range(GRID)] for j in range(step)]
    exchange = functools.partial(
        lax.all_to_all,
        axis_name="row",
        split_axis=0,
        concat_axis=0,
        tiled=True,
        axis_index_groups=groups,
    )
    by_column = current.reshape(grid_rows, -1, GRID, channels).transpose(2, 0, 1, 3)
    windows = window_block(
        exchange(by_column), w_query, w_key, w_value, w_out, w_in, w_down
    )
    fast = step == 1 and grid_cols == GRID * GRID and channels % 128 == 0
    if fast:
        returned, framed = central_by_windows(windows)
    else:
        returned = exchange(windows)
    latent_out = returned.transpose(1, 2, 0, 3).reshape(grid_rows, grid_cols, channels)
    if not fast:
        framed = central_by_rows(latent_out, devices)
    cols = framed.shape[1] - 2
    doubled = jnp.repeat(framed, 2, axis=1)[:, 1:-1]
    if fast:
        taps = jnp.stack([doubled[:, v : v + 2 * cols] for v in range(3)])
        return latent_out, up_block(taps, up_kernel)
    doubled = jnp.pad(jnp.repeat(doubled, 2, axis=0), ((1, 1), (0, 0), (0, 0)))
    total_rows = doubled.shape[0] - 2
    upsampled = convolve(doubled, up_kernel, total_rows, 2 * cols).astype(BF16)
    return latent_out, upsampled.reshape(total_rows, 2 * cols, channels)


def solution(mesh):
    placed = (
        P(("parts", "row"), None, None),
        P(None, None, "row", None),
        P(None, None, "row", None),
        P(),
        P(),
        P(),
        P(),
        P(),
        P(),
        P(None, None, "row", None),
    )
    return jax.shard_map(
        on_device,
        mesh=mesh,
        in_specs=placed,
        out_specs=(P(("parts", "row"), None, None), P("parts", "row", None)),
        check_vma=False,
    )
```
